32 devices in a mesh: pipe: 4 (over x, core), dp: 8 (over z, y).
Axes of the slice: x: 2, y: 2, z: 4, core: 2. Of those that a mesh axis runs over, the one named last changes fastest.
Arguments:
- saved_inputs: bfloat16 [4, 4096, 896], P('pipe', 'dp'), may hold values from -6 to 6
- projections: bfloat16 [4, 896, 1792], P('pipe', 'dp'), may hold values from -0.09375 to 0.09375
- mixing: bfloat16 [4, 16, 8, 256, 256], P('pipe', 'dp'), may hold values from -0.375 to 0.375
- out_cotangent: bfloat16 [4096, 896], P('dp'), may hold values from -6 to 6
Outputs:
- section_cotangents: bfloat16 [4, 4096, 896], P('pipe', 'dp')
- weight_grads: float32 [4, 896, 1792], P('pipe', 'dp')
The draws below stay inside these ranges and needn't reach their ends.
All inputs are finite; a program needn't handle non-finite values.
Results may differ from the reference program's by a relative error of at most 0.028.
Values may be sent and summed in bfloat16 or wider, within the bound.
A program may use at most 64 MiB of HBM per device.

```python
import jax
import jax.numpy as jnp
from jax import lax

DW = 896
HEADS = 8
PATCHES = 256
HD = 896
IMAGES = 16
ROWS = 4096
N_PIPE = 4
N_DP = 8


def spiked(drawn, key, source, target, parts, factor):
    def block_of(axis_at):
        return (jnp.arange(drawn.shape[axis_at]) // (drawn.shape[axis_at] // parts)).reshape((-1,) + (1,) * (drawn.ndim - 1 - axis_at))

    first = jax.random.permutation(key, parts)[block_of(target)]
    far = (block_of(target) + parts // 2) % parts
    return jnp.where((block_of(source) == first) | (block_of(source) == far), factor * drawn, drawn)


def block_levels(rng, shape, cuts, low, largest):
    level, own = 1.0, jax.random.fold_in(rng, 6)
    for position, shards_of in cuts:
        steps = jnp.exp(jax.random.uniform(jax.random.fold_in(own, position), (shards_of,), jnp.float32, low / len(cuts), largest / len(cuts)))
        level = level * jnp.repeat(steps, shape[position] // shards_of).reshape([-1 if axis == position else 1 for axis in range(len(shape))])
    return level


def scatter_about(stream_key, shape, spread, limit, cuts=(), dtype=jnp.bfloat16):
    drawn = spread * jax.random.normal(stream_key, shape, jnp.float32)
    if cuts:
        drawn = drawn * block_levels(stream_key, shape, cuts, -0.22, 0.18)
    return jnp.clip(drawn, -limit, limit).astype(dtype)


def heavy_noise(rng, shape, scale, bound, split, heavy, dtype=jnp.bfloat16):
    drawn = scale * jax.random.normal(rng, shape, jnp.float32)
    if split:
        drawn = drawn * block_levels(rng, shape, split, -0.22, 0.18)
    return jnp.clip(spiked(drawn, jax.random.fold_in(rng, 3), *heavy), -bound, bound).astype(dtype)


def setup_inputs(seed: int = 0) -> dict:
    splits = jax.random.split(jax.random.key(seed), 5)
    return {
        "saved_inputs": heavy_noise(splits[0], (N_PIPE, ROWS, DW), 1.0, 6.0, ((0, 4), (1, 8)), (1, 2, 8, 2.0)),
        "projections": scatter_about(splits[1], (N_PIPE, DW, 2 * HD), (4 * DW) ** -0.5, 0.09375, ((0, 4), (1, 8))),
        "mixing": scatter_about(splits[2], (N_PIPE, IMAGES, HEADS, PATCHES, PATCHES), PATCHES ** -0.5, 0.375, ((0, 4), (1, 8))),
        "out_cotangent": scatter_about(splits[3], (ROWS, DW), 1.0, 6.0, ((0, 8),)),
    }


FORWARD = 'bhij,bjhd->bihd'
BACKWARD = 'bhij,bihd->bjhd'

def normalize(row_block):
    widened = row_block.astype(jnp.float32)
    centred = widened - lax.optimization_barrier(jnp.mean(widened, axis=-1, keepdims=True))
    inverse = lax.rsqrt(lax.optimization_barrier(jnp.mean(centred * centred, axis=-1, keepdims=True)) + 1e-06)
    return (centred * inverse, inverse)

def mix_heads(weights, row_block, pattern):
    images, head_count, patches = (weights.shape[0], weights.shape[1], weights.shape[2])
    per_head = row_block.reshape(images, patches, head_count, -1).astype(jnp.float32)
    mixed_rows = jnp.einsum(pattern, weights.astype(jnp.float32), per_head)
    return mixed_rows.reshape(images * patches, -1).astype(jnp.bfloat16)

def norm_backward(cotangent, d_normed, scaled, inverse):
    inner = d_normed - lax.optimization_barrier(jnp.mean(d_normed, axis=-1, keepdims=True)) - scaled * lax.optimization_barrier(jnp.mean(d_normed * scaled, axis=-1, keepdims=True))
    return (cotangent.astype(jnp.float32) + inverse * inner).astype(jnp.bfloat16)

def replica_sums(normed, d_values, cotangent, context):

    def replica_term(pieces):
        normed_rows, dvalue_rows, cot_rows, context_rows = pieces
        grad_block = jnp.concatenate([jnp.dot(normed_rows.T, dvalue_rows, preferred_element_type=jnp.float32), jnp.dot(cot_rows.T, context_rows, preferred_element_type=jnp.float32)], axis=1)
        rounded = lax.optimization_barrier(grad_block.astype(jnp.bfloat16))
        return rounded.astype(jnp.float32)
    pieces = (normed.reshape(N_DP, -1, DW), d_values.reshape(N_DP, -1, HD), cotangent.reshape(N_DP, -1, DW), context.reshape(N_DP, -1, HD))
    return lax.optimization_barrier(jnp.sum(lax.map(replica_term, pieces), axis=0))

def reference(saved_inputs, projections, mixing, out_cotangent):
    section_count = saved_inputs.shape[0]
    cotangent = out_cotangent
    section_list = []
    grad_list = []
    for section_id in range(section_count - 1, -1, -1):
        value_weight = projections[section_id][:, :HD]
        output_weight = projections[section_id][:, HD:]
        scaled, inverse = normalize(saved_inputs[section_id])
        normed = scaled.astype(jnp.bfloat16)
        values = jnp.dot(normed, value_weight, preferred_element_type=jnp.float32).astype(jnp.bfloat16)
        context = mix_heads(mixing[section_id], values, FORWARD)
        d_context = jnp.dot(cotangent, output_weight, preferred_element_type=jnp.float32).astype(jnp.bfloat16)
        d_values = mix_heads(mixing[section_id], d_context, BACKWARD)
        d_normed = jnp.dot(d_values, value_weight.T, preferred_element_type=jnp.float32)
        input_grad = norm_backward(cotangent, d_normed, scaled, inverse)
        grad_list.insert(0, replica_sums(normed, d_values, cotangent, context))
        section_list.insert(0, input_grad)
        cotangent = input_grad
    return (jnp.stack(section_list), jnp.stack(grad_list))
```

```python
import functools

import jax
import jax.numpy as jnp
from jax import lax
from jax.experimental import pallas as pl
from jax.experimental.pallas import tpu as pltpu
from jax.sharding import PartitionSpec as P

FORWARD = "bhij,bjhd->bihd"
BACKWARD = "bhij,bihd->bjhd"


def from_behind(value, axis, by):
    length = lax.axis_size(axis)
    pairs = [(i, i + by) for i in range(length) if 0 <= i + by < length]
    return lax.ppermute(value, axis, pairs)


def normalize(row_block):
    widened = row_block.astype(jnp.float32)
    centred = widened - jnp.mean(widened, axis=-1, keepdims=True)
    inverse = lax.rsqrt(jnp.mean(centred * centred, axis=-1, keepdims=True) + 1e-06)
    return (centred * inverse, inverse)


def mix_heads(weights, row_block, pattern):
    images, head_count, patches = (weights.shape[0], weights.shape[1], weights.shape[2])
    per_head = row_block.reshape(images, patches, head_count, -1)
    mixed_rows = jnp.einsum(pattern, weights, per_head, preferred_element_type=jnp.float32)
    return mixed_rows.reshape(images * patches, -1).astype(jnp.bfloat16)


def norm_backward(cotangent, d_normed, scaled, inverse):
    inner = (
        d_normed
        - jnp.mean(d_normed, axis=-1, keepdims=True)
        - scaled * jnp.mean(d_normed * scaled, axis=-1, keepdims=True)
    )
    return (cotangent.astype(jnp.float32) + inverse * inner).astype(jnp.bfloat16)


def row_product(left, right):
    return lax.dot_general(
        left, right, (((0,), (0,)), ((), ())), preferred_element_type=jnp.float32
    )


def body(saved_inputs, projections, mixing, out_cotangent):
    section_count = lax.axis_size("pipe")
    section_id = lax.axis_index("pipe")
    inputs = saved_inputs[0]
    mixes = mixing[0]
    micro_count = mixes.shape[0]
    patches = mixes.shape[-1]
    width = inputs.shape[1]
    gathered = lax.all_gather(projections[0], "dp", axis=0, tiled=True)
    head_cols = gathered.shape[1] // 2
    value_weight = gathered[:, :head_cols]
    output_weight = gathered[:, head_cols:]
    total_rows = inputs.shape[0]

    def input_side(row_block, mix_block, cotangent):
        scaled, inverse = normalize(row_block)
        d_context = jnp.dot(cotangent, output_weight, preferred_element_type=jnp.float32).astype(
            jnp.bfloat16
        )
        d_values = mix_heads(mix_block, d_context, BACKWARD)
        d_normed = lax.dot_general(
            d_values, value_weight, (((1,), (1,)), ((), ())), preferred_element_type=jnp.float32
        )
        return (
            scaled.astype(jnp.bfloat16),
            d_values,
            norm_backward(cotangent, d_normed, scaled, inverse),
        )

    cot_buffer = jnp.zeros((total_rows, width), jnp.bfloat16)
    carried = (
        cot_buffer,
        jnp.zeros((total_rows, width), jnp.bfloat16),
        jnp.zeros((total_rows, width), jnp.bfloat16),
        jnp.zeros((total_rows, head_cols), jnp.bfloat16),
    )

    def active_step(holding, row_start, mix_block, cotangent):
        row_block = lax.dynamic_slice_in_dim(inputs, row_start, patches, 0)
        normed, d_values, input_grad = input_side(row_block, mix_block, cotangent)
        pieces = (input_grad, normed, cotangent, d_values)
        updated = tuple(
            (
                lax.dynamic_update_slice_in_dim(buffer, piece, row_start, 0)
                for buffer, piece in zip(holding, pieces)
            )
        )
        return (updated, input_grad)

    def advance(instant, loop_state):
        incoming, holding = loop_state
        position = instant - (section_count - 1 - section_id)
        active = jnp.logical_and(position >= 0, position < micro_count)
        clamped = jnp.clip(position, 0, micro_count - 1)
        row_start = clamped * patches
        fresh_rows = lax.dynamic_slice_in_dim(out_cotangent, row_start, patches, 0)
        cotangent = jnp.where(section_id == section_count - 1, fresh_rows, incoming)
        mix_block = lax.dynamic_slice_in_dim(mixes, clamped, 1, 0)

        def run_step(state_now):
            return active_step(state_now, row_start, mix_block, cotangent)

        def empty_step(state_now):
            return (state_now, jnp.zeros_like(cotangent))

        holding, input_grad = lax.cond(active, run_step, empty_step, holding)
        incoming = from_behind(input_grad, "pipe", -1)
        return (incoming, holding)

    start_state = (jnp.zeros((patches, width), jnp.bfloat16), carried)
    incoming, carried = lax.fori_loop(0, section_count + micro_count - 1, advance, start_state)
    section_grads, normed_all, cotangents_all, d_values_all = carried
    values_all = jnp.dot(normed_all, value_weight, preferred_element_type=jnp.float32).astype(
        jnp.bfloat16
    )
    context_all = mix_heads(mixes, values_all, FORWARD)
    weight_grads = lax.psum_scatter(
        jnp.concatenate(
            [row_product(normed_all, d_values_all), row_product(cotangents_all, context_all)],
            axis=1,
        ).astype(jnp.bfloat16),
        "dp",
        scatter_dimension=0,
        tiled=True,
    ).astype(jnp.float32)
    return (section_grads[None], weight_grads[None])


LANES = 128
MESH = pl.DeviceIdType.MESH


def ring_index(position, length):
    return jnp.where(position < length // 2, 2 * position, 2 * (length - 1 - position) + 1)


GATE = 1
PIECE = 256
FORWARD_OP, CONTEXT_OP, MIX_OP, INPUT_OP, COT_GRAD_OP, NORM_GRAD_OP, ARRIVAL_OP = range(7)
SLOT = 1024
OP_SIZE = 128


def schedules(images, pieces):
    def context(b):
        return [(CONTEXT_OP, c) for c in range(b * pieces, (b + 1) * pieces)]

    def inputs(b):
        return [(INPUT_OP, c) for c in range(b * pieces, (b + 1) * pieces)]

    def each(op):
        return [(op, b) for b in range(images)]

    arrival, end = [(ARRIVAL_OP, 0)], images - 1
    mixed = [step for b in range(images) for step in context(b) + [(MIX_OP, b)]]
    sent = [step for b in range(images) for step in inputs(b)]
    early = mixed + arrival + sent + each(FORWARD_OP) + each(COT_GRAD_OP) + each(NORM_GRAD_OP)
    middle = arrival + each(FORWARD_OP) + context(0)
    final = arrival + each(FORWARD_OP) + context(0)
    kept = []
    for b in range(end):
        later = context(b + 1)
        middle += [(MIX_OP, b)] + inputs(b) + [(COT_GRAD_OP, b)] + later[:-1]
        middle += [(NORM_GRAD_OP, b)] + later[-1:]
        final += [(COT_GRAD_OP, b), (MIX_OP, b), (NORM_GRAD_OP, b)] + later
        kept += inputs(b)
    middle += [(COT_GRAD_OP, end), (MIX_OP, end)] + inputs(end) + [(NORM_GRAD_OP, end)]
    final += [(COT_GRAD_OP, end), (MIX_OP, end), (NORM_GRAD_OP, end)] + kept + inputs(end)
    return early, middle, final


def packed(steps):
    codes = [op * OP_SIZE + argument for op, argument in steps]
    codes += [0] * (-len(codes) % 3)
    return [
        codes[i] + codes[i + 1] * SLOT + codes[i + 2] * SLOT * SLOT
        for i in range(0, len(codes), 3)
    ]


def fused_kernel(
    x_hbm, w_hbm, mix_hbm, oc_hbm, sc_hbm, wg_hbm,
    x_ref, mix_ref, sc_ref, wg_ref, sums, weights, scaled, inverse, normed, lefts, rights, mix_t, cot, d_ctx, vals, partial, landing,
    ag_send, ag_recv, rs_send, rs_recv, cot_send, cot_recv, load_sem, sc_sem, wg_sem, go_sem,
):
    n = lax.axis_size("dp")
    sections = lax.axis_size("pipe")
    me = lax.axis_index("dp")
    s = lax.axis_index("pipe")
    place = jnp.where(lax.rem(me, 2) == 0, me // 2, n - 1 - me // 2)
    up = ring_index(lax.rem(place + 1, n), n)
    down = ring_index(lax.rem(place + n - 1, n), n)
    share = w_hbm.shape[0]
    width, both = weights.shape
    hd = both // 2
    images, heads, patches = mix_ref.shape[:3]
    pieces = patches // PIECE
    hops = n // 2
    tiles = hd // LANES
    near = (tiles + 1) // 2 * LANES
    far = hd - near

    last = s == sections - 1
    leads = lax.rem(s, 2) == 1
    partner = jnp.where(leads, s - 1, s + 1)

    def rows_of(position):
        return pl.ds(pl.multiple_of(ring_index(position, n) * share, 16), share)

    load_w = pltpu.make_async_copy(w_hbm, weights.at[rows_of(place), :], load_sem.at[3])
    load_x = pltpu.make_async_copy(x_hbm, x_ref, load_sem.at[0])
    load_mix = pltpu.make_async_copy(mix_hbm, mix_ref, load_sem.at[1])
    load_cot = pltpu.make_async_copy(oc_hbm, cot, load_sem.at[2])

    load_w.start()
    barrier = pltpu.get_barrier_semaphore()
    for target in ({"dp": up}, {"dp": down}):
        pl.semaphore_signal(barrier, inc=1, device_id=target, device_id_type=MESH)
    for step in (1, sections - 1):
        pl.semaphore_signal(
            barrier, inc=1, device_id={"pipe": lax.rem(s + step, sections)}, device_id_type=MESH
        )
    pl.semaphore_wait(barrier, 4)

    def tell_partner():
        pl.semaphore_signal(go_sem, inc=1, device_id={"pipe": partner}, device_id_type=MESH)

    streams = []
    for half in (1, 0):
        for first, count in ((0, near), (near, far)):
            for direction in (1, -1):
                whole = (first == 0) == ((direction == 1) == (half == 1))
                streams.append((direction, half, first, count, whole))
    lanes_of = range(len(streams))
    output_lanes, value_lanes = lanes_of[:4], lanes_of[4:]

    def ag_copy(k, t, arriving):
        direction, half, first, count, _ = streams[k]
        offset = t + 1 if arriving else t
        position = lax.rem(place - direction * offset + 2 * n, n)
        block = weights.at[rows_of(position), pl.ds(half * hd + first, count)]
        return pltpu.make_async_remote_copy(
            src_ref=block, dst_ref=block,
            send_sem=ag_send.at[k, t], recv_sem=ag_recv.at[k, t],
            device_id={"dp": up if direction == 1 else down}, device_id_type=MESH,
        )

    def travels(k, t):
        return t < (hops if streams[k][4] else hops - 1)

    load_x.start()
    load_mix.start()

    @pl.when(last)
    def _():
        load_cot.start()

    load_w.wait()

    @pl.when(jnp.logical_not(leads))
    def _():
        pl.semaphore_wait(go_sem, 1)

    for k in lanes_of:
        ag_copy(k, 0, False).start()

    def prepare_rows(u):
        rows = pl.ds(pl.multiple_of(u * LANES, LANES), LANES)
        wide = x_ref[rows, :].astype(jnp.float32)
        centred = wide - jnp.mean(wide, axis=-1, keepdims=True)
        inv = lax.rsqrt(jnp.mean(centred * centred, axis=-1, keepdims=True) + 1e-06)
        unit = centred * inv
        scaled[rows, :] = unit
        inverse[rows, :] = inv
        rounded = unit.astype(jnp.bfloat16)
        normed[rows, :] = rounded
        lefts[0, :, rows] = rounded.T

    def prepare_mix(u):
        b, h = u // heads, lax.rem(u, heads)
        mix_t[b, h] = mix_ref[b, h].T

    def prepare(t):
        for count, work in ((x_ref.shape[0] // LANES, prepare_rows), (images * heads, prepare_mix)):
            pl.loop(t * count // (hops - 1), (t + 1) * count // (hops - 1))(work)

    load_x.wait()
    load_mix.wait()

    @pl.when(last)
    def _():
        load_cot.wait()

    @pl.loop(0, hops - 1)
    def _(t):
        for k in lanes_of:
            ag_copy(k, t, True).wait_recv()

            @pl.when(travels(k, t + 1))
            def _():
                ag_copy(k, t + 1, False).start()

        @pl.when(jnp.logical_and(leads, t == GATE))
        def _():
            tell_partner()

        prepare(t)

    def arrive(lanes):
        for k in lanes:
            if streams[k][4]:
                ag_copy(k, hops - 1, True).wait_recv()

    arrive(output_lanes)

    head_width = hd // heads
    lane = lax.broadcasted_iota(jnp.int32, (patches, LANES), 1)

    def mix_rows(matrices, b, source, dest, rows):
        made = {}
        for h in range(heads):
            low, high = h * head_width // LANES, ((h + 1) * head_width - 1) // LANES
            product = jnp.dot(
                matrices[b, h],
                source[rows, low * LANES : (high + 1) * LANES],
                preferred_element_type=jnp.float32,
            )
            for tile in range(low, high + 1):
                piece = product[:, (tile - low) * LANES : (tile - low + 1) * LANES]
                begin = h * head_width - tile * LANES
                made[tile] = piece if tile not in made else jnp.where(lane < begin, made[tile], piece)
                if (h + 1) * head_width >= (tile + 1) * LANES:
                    dest[rows, tile * LANES : (tile + 1) * LANES] = made[tile].astype(jnp.bfloat16)

    def image_rows(b):
        return pl.ds(pl.multiple_of(b * patches, patches), patches)

    def piece_rows(c):
        return pl.ds(pl.multiple_of(c * PIECE, PIECE), PIECE)

    def cot_copy(c):
        rows = piece_rows(c)
        return pltpu.make_async_remote_copy(
            src_ref=sc_ref.at[rows, :], dst_ref=cot.at[rows, :],
            send_sem=cot_send.at[c], recv_sem=cot_recv.at[c],
            device_id={"pipe": lax.rem(s + sections - 1, sections)}, device_id_type=MESH,
        )

    d_values, context = rights.at[0], rights.at[1]

    def sc_copy(c):
        rows = piece_rows(c)
        return pltpu.make_async_copy(sc_ref.at[rows, :], sc_hbm.at[rows, :], sc_sem.at[c])

    def forward(b):
        rows = image_rows(b)
        vals[rows, :] = jnp.dot(
            normed[rows, :], weights[:, :hd], preferred_element_type=jnp.float32
        ).astype(jnp.bfloat16)
        mix_rows(mix_ref, b, vals, context, rows)

    def to_context(c):
        rows = piece_rows(c)

        @pl.when(jnp.logical_not(last))
        def _():
            cot_copy(c).wait_recv()

        d_ctx[rows, :] = jnp.dot(
            cot[rows, :], weights[:, hd:], preferred_element_type=jnp.float32
        ).astype(jnp.bfloat16)
        lefts[1, :, rows] = cot[rows, :].T

    def to_values(b):
        mix_rows(mix_t, b, d_ctx, d_values, image_rows(b))

    def to_input(c):
        rows = piece_rows(c)
        d_normed = lax.dot_general(
            d_values[rows, :], weights[:, :hd], (((1,), (1,)), ((), ())),
            preferred_element_type=jnp.float32,
        )
        unit = scaled[rows, :]
        inner = (
            d_normed
            - jnp.mean(d_normed, axis=-1, keepdims=True)
            - unit * jnp.mean(d_normed * unit, axis=-1, keepdims=True)
        )
        sc_ref[rows, :] = (cot[rows, :].astype(jnp.float32) + inverse[rows, :] * inner).astype(jnp.bfloat16)

        @pl.when(s > 0)
        def _():
            cot_copy(c).start()

        sc_copy(c).start()

    def arrival(_):
        arrive(value_lanes)

        @pl.when(jnp.logical_not(leads))
        def _():
            tell_partner()

    def wg_copy(k):
        _, half, first, count, _ = streams[k]
        columns = pl.ds(half * hd + first, count)
        return pltpu.make_async_copy(wg_ref.at[:, columns], wg_hbm.at[:, columns], wg_sem.at[k])

    def ahead(direction, distance):
        return rows_of(lax.rem(place + direction * distance + n, n))

    def rs_copy(k, t, first_leg=False):
        direction, half, first, count, _ = streams[k]
        columns = pl.ds(first, count)
        side = (1 - direction) // 2
        if first_leg:
            origin = partial.at[half, ahead(direction, hops - t), columns]
        else:
            origin = landing.at[side, half, jnp.maximum(t - 1, 0), :, columns]
        return pltpu.make_async_remote_copy(
            src_ref=origin, dst_ref=landing.at[side, half, t, :, columns],
            send_sem=rs_send.at[k, t], recv_sem=rs_recv.at[k, t],
            device_id={"dp": up if direction == 1 else down}, device_id_type=MESH,
        )

    def send_partials(lanes):
        for k in sorted(lanes, key=lambda k: not streams[k][4]):
            rs_copy(k, 0 if streams[k][4] else 1, True).start()

    part = width // 2

    def gradients(half, b):
        rows = image_rows(b)

        @pl.loop(0, 2)
        def _(i):
            block = pl.ds(pl.multiple_of(i * part, 16), part)
            term = jnp.dot(
                lefts[half, block, rows], rights[half, rows, :],
                preferred_element_type=jnp.float32,
            )

            @pl.when(jnp.logical_and(b == 0, b < images - 1))
            def _():
                sums[half, block, :] = term

            @pl.when(jnp.logical_and(b > 0, b < images - 1))
            def _():
                sums[half, block, :] += term

            @pl.when(b == images - 1)
            def _():
                total = term if images == 1 else sums[half, block, :] + term
                partial[half, block, :] = total.astype(jnp.bfloat16)

    def cot_gradient(b):
        gradients(1, b)

        @pl.when(b == images - 1)
        def _():
            @pl.when(leads)
            def _():
                pl.semaphore_wait(go_sem, 1)

            send_partials(output_lanes)

    def norm_gradient(b):
        gradients(0, b)

        @pl.when(b == images - 1)
        def _():
            send_partials(value_lanes)

    early, middle, final = (packed(steps) for steps in schedules(images, pieces))
    words = [
        jnp.where(s == 0, c, jnp.where(jnp.logical_and(leads, jnp.logical_not(last)), b, a))
        for a, b, c in zip(early, middle, final)
    ]
    actions = (forward, to_context, to_values, to_input, cot_gradient, norm_gradient, arrival)

    @pl.loop(0, len(schedules(images, pieces)[0]))
    def _(i):
        group, slot = i // 3, lax.rem(i, 3)
        word = words[0]
        for j in range(1, len(words)):
            word = jnp.where(group == j, words[j], word)
        code = jnp.where(slot == 0, word, jnp.where(slot == 1, word // SLOT, word // (SLOT * SLOT)))
        code = lax.rem(code, SLOT)
        work, argument = code // OP_SIZE, lax.rem(code, OP_SIZE)
        for number, action in enumerate(actions):
            pl.when(work == number)(functools.partial(action, argument))

    @pl.loop(1, hops)
    def _(t):
        def add_on(k):
            direction, half, first, count, _ = streams[k]
            columns = pl.ds(first, count)
            side = (1 - direction) // 2
            rs_copy(k, t - 1).wait_recv()
            total = landing[side, half, t - 1, :, columns].astype(jnp.float32) + partial[
                half, ahead(direction, hops - t), columns
            ].astype(jnp.float32)
            landing[side, half, t - 1, :, columns] = total.astype(jnp.bfloat16)
            rs_copy(k, t).start()

        for k in lanes_of:
            if streams[k][4]:
                add_on(k)
            else:
                pl.when(t > 1)(functools.partial(add_on, k))

    for k in lanes_of[::2]:
        _, half, first, count, _ = streams[k]
        columns = pl.ds(first, count)
        total = partial[half, rows_of(place), columns].astype(jnp.float32)
        for side in range(2):
            rs_copy(k + side, hops - 1).wait_recv()
            total += landing[side, half, hops - 1, :, columns].astype(jnp.float32)
        wg_ref[:, pl.ds(half * hd + first, count)] = total
        wg_copy(k).start()

    @pl.loop(0, hops)
    def _(t):
        for k in lanes_of:
            pl.when(travels(k, t))(lambda: ag_copy(k, t, False).wait_send())
            pl.when(travels(k, hops - 1 - t))(lambda: rs_copy(k, t).wait_send())

    @pl.when(s > 0)
    def _():
        @pl.loop(0, images * pieces)
        def _(c):
            cot_copy(c).wait_send()

    @pl.loop(0, images * pieces)
    def _(c):
        sc_copy(c).wait()

    for k in lanes_of[::2]:
        wg_copy(k).wait()


def fused_body(saved_inputs, projections, mixing, out_cotangent):
    n = lax.axis_size("dp")
    rows, width = out_cotangent.shape
    share, both = projections.shape[1:]
    hd = both // 2
    images, heads, patches = mixing.shape[1:4]
    bf16, f32 = jnp.bfloat16, jnp.float32
    hbm = pl.BlockSpec(memory_space=pl.ANY)
    section_grads, weight_grads = pl.pallas_call(
        fused_kernel,
        out_shape=(
            jax.ShapeDtypeStruct((rows, width), bf16),
            jax.ShapeDtypeStruct((share, both), f32),
        ),
        in_specs=[hbm] * 4,
        out_specs=(hbm, hbm),
        scratch_shapes=[
            pltpu.VMEM((rows, width), bf16),
            pltpu.VMEM((images, heads, patches, patches), bf16),
            pltpu.VMEM((rows, width), bf16),
            pltpu.VMEM((share, both), f32),
            pltpu.VMEM((2, width, hd), f32),
            pltpu.VMEM((width, both), bf16),
            pltpu.VMEM((rows, width), f32),
            pltpu.VMEM((rows, 1), f32),
            pltpu.VMEM((rows, width), bf16),
            pltpu.VMEM((2, width, rows), bf16),
            pltpu.VMEM((2, rows, hd), bf16),
            pltpu.VMEM((images, heads, patches, patches), bf16),
            pltpu.VMEM((rows, width), bf16),
            pltpu.VMEM((rows, hd), bf16),
            pltpu.VMEM((rows, hd), bf16),
            pltpu.VMEM((2, width, hd), bf16),
            pltpu.VMEM((2, 2, n // 2, share, hd), bf16),
            pltpu.SemaphoreType.DMA((8, n // 2)),
            pltpu.SemaphoreType.DMA((8, n // 2)),
            pltpu.SemaphoreType.DMA((8, n // 2)),
            pltpu.SemaphoreType.DMA((8, n // 2)),
            pltpu.SemaphoreType.DMA((rows // LANES,)),
            pltpu.SemaphoreType.DMA((rows // LANES,)),
            pltpu.SemaphoreType.DMA((4,)),
            pltpu.SemaphoreType.DMA((rows // LANES,)),
            pltpu.SemaphoreType.DMA((8,)),
            pltpu.SemaphoreType.REGULAR,
        ],
        compiler_params=pltpu.CompilerParams(
            collective_id=0, has_side_effects=True, vmem_limit_bytes=48 * 1024 * 1024
        ),
    )(*(pltpu.with_memory_space_constraint(a, pltpu.HBM) for a in (saved_inputs[0], projections[0], mixing[0], out_cotangent)))
    return (section_grads[None], weight_grads[None])


def any_body(saved_inputs, projections, mixing, out_cotangent):
    share, both = projections.shape[1:]
    width = saved_inputs.shape[2]
    n = lax.axis_size("dp")
    aligned = (
        share % 16 == 0
        and both % (2 * LANES) == 0
        and width % LANES == 0
        and mixing.shape[3] % PIECE == 0
        and n % 2 == 0
        and n > 2
        and lax.axis_size("pipe") > 2
        and lax.axis_size("pipe") % 2 == 0
        and out_cotangent.shape[0] < OP_SIZE * LANES
    )
    chosen = fused_body if aligned else body
    return chosen(saved_inputs, projections, mixing, out_cotangent)


def solution(mesh):
    return jax.shard_map(
        any_body,
        mesh=mesh,
        in_specs=(
            P("pipe", "dp", None),
            P("pipe", "dp", None),
            P("pipe", "dp", None, None, None),
            P("dp", None),
        ),
        out_specs=(P("pipe", "dp", None), P("pipe", "dp", None)),
        check_vma=False,
    )
```

```python
import functools

import jax
import jax.numpy as jnp
from jax import lax
from jax.experimental import pallas as pl
from jax.experimental.pallas import tpu as pltpu
from jax.sharding import PartitionSpec as P

FORWARD = "bhij,bjhd->bihd"
BACKWARD = "bhij,bihd->bjhd"


def from_behind(value, axis, by):
    length = lax.axis_size(axis)
    pairs = [(i, i + by) for i in range(length) if 0 <= i + by < length]
    return lax.ppermute(value, axis, pairs)


def normalize(row_block):
    widened = row_block.astype(jnp.float32)
    centred = widened - jnp.mean(widened, axis=-1, keepdims=True)
    inverse = lax.rsqrt(jnp.mean(centred * centred, axis=-1, keepdims=True) + 1e-06)
    return (centred * inverse, inverse)


def mix_heads(weights, row_block, pattern):
    images, head_count, patches = (weights.shape[0], weights.shape[1], weights.shape[2])
    per_head = row_block.reshape(images, patches, head_count, -1)
    mixed_rows = jnp.einsum(pattern, weights, per_head, preferred_element_type=jnp.float32)
    return mixed_rows.reshape(images * patches, -1).astype(jnp.bfloat16)


def norm_backward(cotangent, d_normed, scaled, inverse):
    inner = (
        d_normed
        - jnp.mean(d_normed, axis=-1, keepdims=True)
        - scaled * jnp.mean(d_normed * scaled, axis=-1, keepdims=True)
    )
    return (cotangent.astype(jnp.float32) + inverse * inner).astype(jnp.bfloat16)


def row_product(left, right):
    return lax.dot_general(
        left, right, (((0,), (0,)), ((), ())), preferred_element_type=jnp.float32
    )


def body(saved_inputs, projections, mixing, out_cotangent):
    section_count = lax.axis_size("pipe")
    section_id = lax.axis_index("pipe")
    inputs = saved_inputs[0]
    mixes = mixing[0]
    micro_count = mixes.shape[0]
    patches = mixes.shape[-1]
    width = inputs.shape[1]
    gathered = lax.all_gather(projections[0], "dp", axis=0, tiled=True)
    head_cols = gathered.shape[1] // 2
    value_weight = gathered[:, :head_cols]
    output_weight = gathered[:, head_cols:]
    total_rows = inputs.shape[0]

    def input_side(row_block, mix_block, cotangent):
        scaled, inverse = normalize(row_block)
        d_context = jnp.dot(cotangent, output_weight, preferred_element_type=jnp.float32).astype(
            jnp.bfloat16
        )
        d_values = mix_heads(mix_block, d_context, BACKWARD)
        d_normed = lax.dot_general(
            d_values, value_weight, (((1,), (1,)), ((), ())), preferred_element_type=jnp.float32
        )
        return (
            scaled.astype(jnp.bfloat16),
            d_values,
            norm_backward(cotangent, d_normed, scaled, inverse),
        )

    cot_buffer = jnp.zeros((total_rows, width), jnp.bfloat16)
    carried = (
        cot_buffer,
        jnp.zeros((total_rows, width), jnp.bfloat16),
        jnp.zeros((total_rows, width), jnp.bfloat16),
        jnp.zeros((total_rows, head_cols), jnp.bfloat16),
    )

    def active_step(holding, row_start, mix_block, cotangent):
        row_block = lax.dynamic_slice_in_dim(inputs, row_start, patches, 0)
        normed, d_values, input_grad = input_side(row_block, mix_block, cotangent)
        pieces = (input_grad, normed, cotangent, d_values)
        updated = tuple(
            (
                lax.dynamic_update_slice_in_dim(buffer, piece, row_start, 0)
                for buffer, piece in zip(holding, pieces)
            )
        )
        return (updated, input_grad)

    def advance(instant, loop_state):
        incoming, holding = loop_state
        position = instant - (section_count - 1 - section_id)
        active = jnp.logical_and(position >= 0, position < micro_count)
        clamped = jnp.clip(position, 0, micro_count - 1)
        row_start = clamped * patches
        fresh_rows = lax.dynamic_slice_in_dim(out_cotangent, row_start, patches, 0)
        cotangent = jnp.where(section_id == section_count - 1, fresh_rows, incoming)
        mix_block = lax.dynamic_slice_in_dim(mixes, clamped, 1, 0)

        def run_step(state_now):
            return active_step(state_now, row_start, mix_block, cotangent)

        def empty_step(state_now):
            return (state_now, jnp.zeros_like(cotangent))

        holding, input_grad = lax.cond(active, run_step, empty_step, holding)
        incoming = from_behind(input_grad, "pipe", -1)
        return (incoming, holding)

    start_state = (jnp.zeros((patches, width), jnp.bfloat16), carried)
    incoming, carried = lax.fori_loop(0, section_count + micro_count - 1, advance, start_state)
    section_grads, normed_all, cotangents_all, d_values_all = carried
    values_all = jnp.dot(normed_all, value_weight, preferred_element_type=jnp.float32).astype(
        jnp.bfloat16
    )
    context_all = mix_heads(mixes, values_all, FORWARD)
    weight_grads = lax.psum_scatter(
        jnp.concatenate(
            [row_product(normed_all, d_values_all), row_product(cotangents_all, context_all)],
            axis=1,
        ).astype(jnp.bfloat16),
        "dp",
        scatter_dimension=0,
        tiled=True,
    ).astype(jnp.float32)
    return (section_grads[None], weight_grads[None])


LANES = 128
MESH = pl.DeviceIdType.MESH


def ring_index(position, length):
    return jnp.where(position < length // 2, 2 * position, 2 * (length - 1 - position) + 1)


GATE = 0
FORWARD_OP, CONTEXT_OP, MIX_OP, INPUT_OP, COT_GRAD_OP, NORM_GRAD_OP, ARRIVAL_OP, RECEIVE_OP = range(8)
SLOT = 1024
OP_SIZE = 128


def schedules(images):
    def each(*ops):
        return [(op, b) for b in range(images) for op in ops]

    arrival, end = [(ARRIVAL_OP, 0)], images - 1
    early = [(op, 0) for op in (RECEIVE_OP, CONTEXT_OP, MIX_OP)] + arrival + [(INPUT_OP, 0)]
    for b in range(1, images):
        early += [(op, b) for op in (RECEIVE_OP, CONTEXT_OP, MIX_OP, INPUT_OP)]
    early += each(FORWARD_OP) + each(COT_GRAD_OP) + each(NORM_GRAD_OP)
    middle = arrival + each(FORWARD_OP)
    for b in range(end):
        middle += [(op, b) for op in (RECEIVE_OP, CONTEXT_OP, MIX_OP, INPUT_OP, COT_GRAD_OP, NORM_GRAD_OP)]
    middle += [
        (op, end) for op in (RECEIVE_OP, COT_GRAD_OP, CONTEXT_OP, MIX_OP, INPUT_OP, NORM_GRAD_OP)
    ]
    final = arrival + each(FORWARD_OP)
    final += each(RECEIVE_OP, COT_GRAD_OP, CONTEXT_OP, MIX_OP, NORM_GRAD_OP) + each(INPUT_OP)
    return early, middle, final


def packed(steps):
    codes = [op * OP_SIZE + argument for op, argument in steps]
    codes += [0] * (-len(codes) % 3)
    return [
        codes[i] + codes[i + 1] * SLOT + codes[i + 2] * SLOT * SLOT
        for i in range(0, len(codes), 3)
    ]


def fused_kernel(
    x_hbm, w_hbm, mix_hbm, oc_hbm, sc_hbm, wg_hbm,
    x_ref, mix_ref, sc_ref, wg_ref, sums, weights, extra, scaled, inverse, normed, lefts, rights, mix_t, cot, d_ctx, vals, partial, landing,
    ag_send, ag_recv, rs_send, rs_recv, cot_send, cot_recv, load_sem, sc_sem, wg_sem, seed_send, seed_recv, ring_send, ring_recv, back_send, back_recv, go_sem,
):
    n = lax.axis_size("dp")
    sections = lax.axis_size("pipe")
    me = lax.axis_index("dp")
    s = lax.axis_index("pipe")
    place = jnp.where(lax.rem(me, 2) == 0, me // 2, n - 1 - me // 2)
    up = ring_index(lax.rem(place + 1, n), n)
    down = ring_index(lax.rem(place + n - 1, n), n)
    share = w_hbm.shape[0]
    width, both = weights.shape
    hd = both // 2
    images, heads, patches = mix_ref.shape[:3]
    hops = n // 2
    tiles = hd // LANES
    near = (tiles + 1) // 2 * LANES
    far = hd - near

    last = s == sections - 1
    leads = lax.rem(s, 2) == 1
    partner = jnp.where(leads, s - 1, s + 1)
    helped = s == sections - 2
    helps = s == sections - 4
    alone = jnp.logical_not(helped)

    def rows_of(position):
        return pl.ds(pl.multiple_of(ring_index(position, n) * share, 16), share)

    load_w = pltpu.make_async_copy(w_hbm, weights.at[rows_of(place), :], load_sem.at[3])
    load_x = pltpu.make_async_copy(x_hbm, x_ref, load_sem.at[0])
    load_mix = pltpu.make_async_copy(mix_hbm, mix_ref, load_sem.at[1])
    load_cot = pltpu.make_async_copy(oc_hbm, cot, load_sem.at[2])

    load_w.start()
    barrier = pltpu.get_barrier_semaphore()
    for target in ({"dp": up}, {"dp": down}):
        pl.semaphore_signal(barrier, inc=1, device_id=target, device_id_type=MESH)
    steps = sorted({1, 2, sections - 2, sections - 1})
    for step in steps:
        pl.semaphore_signal(
            barrier, inc=1, device_id={"pipe": lax.rem(s + step, sections)}, device_id_type=MESH
        )
    pl.semaphore_wait(barrier, 2 + len(steps))

    def tell_partner():
        pl.semaphore_signal(go_sem, inc=1, device_id={"pipe": partner}, device_id_type=MESH)

    streams = []
    for half in (1, 0):
        for first, count in ((0, near), (near, far)):
            for direction in (1, -1):
                whole = (first == 0) == ((direction == 1) == (half == 1))
                streams.append((direction, half, first, count, whole))
    lanes_of = range(len(streams))
    output_lanes, value_lanes = lanes_of[:4], lanes_of[4:]

    def ag_copy(k, t, arriving):
        direction, half, first, count, _ = streams[k]
        offset = t + 1 if arriving else t
        position = lax.rem(place - direction * offset + 2 * n, n)
        block = weights.at[rows_of(position), pl.ds(half * hd + first, count)]
        return pltpu.make_async_remote_copy(
            src_ref=block, dst_ref=block,
            send_sem=ag_send.at[k, t], recv_sem=ag_recv.at[k, t],
            device_id={"dp": up if direction == 1 else down}, device_id_type=MESH,
        )

    def travels(k, t):
        return t < (hops if streams[k][4] else hops - 1)

    load_x.start()
    load_mix.start()

    @pl.when(last)
    def _():
        load_cot.start()

    def ring_copy(k, t, arriving):
        direction, _, first, count, _ = streams[k]
        offset = t + 1 if arriving else t
        position = lax.rem(place - direction * offset + 2 * n, n)
        block = extra.at[rows_of(position), pl.ds(first, count)]
        return pltpu.make_async_remote_copy(
            src_ref=block, dst_ref=block,
            send_sem=ring_send.at[k - 4, t], recv_sem=ring_recv.at[k - 4, t],
            device_id={"dp": up if direction == 1 else down}, device_id_type=MESH,
        )

    def back_copy(k, t):
        direction, _, first, count, _ = streams[k]
        rows = rows_of(lax.rem(place - direction * (t + 1) + 2 * n, n))
        columns = pl.ds(first, count)
        return pltpu.make_async_remote_copy(
            src_ref=extra.at[rows, columns], dst_ref=weights.at[rows, columns],
            send_sem=back_send.at[k - 4, t], recv_sem=back_recv.at[k - 4, t],
            device_id={"pipe": lax.rem(s + 2, sections)}, device_id_type=MESH,
        )

    def seed_copy(k):
        _, _, first, count, _ = streams[k]
        rows, columns = rows_of(place), pl.ds(first, count)
        return pltpu.make_async_remote_copy(
            src_ref=weights.at[rows, columns], dst_ref=extra.at[rows, columns],
            send_sem=seed_send.at[k // 2 - 2], recv_sem=seed_recv.at[k // 2 - 2],
            device_id={"pipe": lax.rem(s + sections - 2, sections)}, device_id_type=MESH,
        )

    def relay(k, t):
        ring_copy(k, t, True).wait_recv()

        @pl.when(travels(k, t + 1))
        def _():
            ring_copy(k, t + 1, False).start()

        back_copy(k, t).start()

    load_w.wait()

    @pl.when(helped)
    def _():
        for k in value_lanes[::2]:
            seed_copy(k).start()

    @pl.when(helps)
    def _():
        for k in value_lanes[::2]:
            seed_copy(k).wait_recv()
            for side in range(2):
                ring_copy(k + side, 0, False).start()

        @pl.loop(0, hops - 1)
        def _(t):
            for k in value_lanes:
                relay(k, t)

    @pl.when(jnp.logical_not(leads))
    def _():
        pl.semaphore_wait(go_sem, 1)

    for k in output_lanes:
        ag_copy(k, 0, False).start()

    @pl.when(alone)
    def _():
        for k in value_lanes:
            ag_copy(k, 0, False).start()

    @pl.when(helps)
    def _():
        for k in value_lanes:
            if streams[k][4]:
                relay(k, hops - 1)

    def prepare_rows(u):
        rows = pl.ds(pl.multiple_of(u * LANES, LANES), LANES)
        wide = x_ref[rows, :].astype(jnp.float32)
        centred = wide - jnp.mean(wide, axis=-1, keepdims=True)
        inv = lax.rsqrt(jnp.mean(centred * centred, axis=-1, keepdims=True) + 1e-06)
        unit = centred * inv
        scaled[rows, :] = unit
        inverse[rows, :] = inv
        rounded = unit.astype(jnp.bfloat16)
        normed[rows, :] = rounded
        lefts[0, :, rows] = rounded.T

    def prepare_mix(u):
        b, h = u // heads, lax.rem(u, heads)
        mix_t[b, h] = mix_ref[b, h].T

    def prepare(t):
        for count, work in ((x_ref.shape[0] // LANES, prepare_rows), (images * heads, prepare_mix)):
            pl.loop(t * count // (hops - 1), (t + 1) * count // (hops - 1))(work)

    load_x.wait()
    load_mix.wait()

    @pl.when(last)
    def _():
        load_cot.wait()

    def pass_on(k, t):
        ag_copy(k, t, True).wait_recv()

        @pl.when(travels(k, t + 1))
        def _():
            ag_copy(k, t + 1, False).start()

    @pl.loop(0, hops - 1)
    def _(t):
        for k in output_lanes:
            pass_on(k, t)

        @pl.when(alone)
        def _():
            for k in value_lanes:
                pass_on(k, t)

        @pl.when(jnp.logical_and(leads, t == GATE))
        def _():
            tell_partner()

        prepare(t)

    def arrive(lanes):
        for k in lanes:
            if streams[k][4]:
                ag_copy(k, hops - 1, True).wait_recv()

    arrive(output_lanes)

    head_width = hd // heads
    lane = lax.broadcasted_iota(jnp.int32, (patches, LANES), 1)

    def mix_rows(matrices, b, source, dest, rows):
        made = {}
        for h in range(heads):
            low, high = h * head_width // LANES, ((h + 1) * head_width - 1) // LANES
            product = jnp.dot(
                matrices[b, h],
                source[rows, low * LANES : (high + 1) * LANES],
                preferred_element_type=jnp.float32,
            )
            for tile in range(low, high + 1):
                piece = product[:, (tile - low) * LANES : (tile - low + 1) * LANES]
                begin = h * head_width - tile * LANES
                made[tile] = piece if tile not in made else jnp.where(lane < begin, made[tile], piece)
                if (h + 1) * head_width >= (tile + 1) * LANES:
                    dest[rows, tile * LANES : (tile + 1) * LANES] = made[tile].astype(jnp.bfloat16)

    def image_rows(b):
        return pl.ds(pl.multiple_of(b * patches, patches), patches)

    def cot_copy(c):
        rows = image_rows(c)
        return pltpu.make_async_remote_copy(
            src_ref=sc_ref.at[rows, :], dst_ref=cot.at[rows, :],
            send_sem=cot_send.at[c], recv_sem=cot_recv.at[c],
            device_id={"pipe": lax.rem(s + sections - 1, sections)}, device_id_type=MESH,
        )

    d_values, context = rights.at[0], rights.at[1]

    def sc_copy(c):
        rows = image_rows(c)
        return pltpu.make_async_copy(sc_ref.at[rows, :], sc_hbm.at[rows, :], sc_sem.at[c])

    def forward(b):
        rows = image_rows(b)
        vals[rows, :] = jnp.dot(
            normed[rows, :], weights[:, :hd], preferred_element_type=jnp.float32
        ).astype(jnp.bfloat16)
        mix_rows(mix_ref, b, vals, context, rows)

    def receive(c):
        rows = image_rows(c)

        @pl.when(jnp.logical_not(last))
        def _():
            cot_copy(c).wait_recv()

        lefts[1, :, rows] = cot[rows, :].T

    def to_context(c):
        rows = image_rows(c)
        d_ctx[rows, :] = jnp.dot(
            cot[rows, :], weights[:, hd:], preferred_element_type=jnp.float32
        ).astype(jnp.bfloat16)

    def to_values(b):
        mix_rows(mix_t, b, d_ctx, d_values, image_rows(b))

    def to_input(c):
        rows = image_rows(c)
        d_normed = lax.dot_general(
            d_values[rows, :], weights[:, :hd], (((1,), (1,)), ((), ())),
            preferred_element_type=jnp.float32,
        )
        unit = scaled[rows, :]
        inner = (
            d_normed
            - jnp.mean(d_normed, axis=-1, keepdims=True)
            - unit * jnp.mean(d_normed * unit, axis=-1, keepdims=True)
        )
        sc_ref[rows, :] = (cot[rows, :].astype(jnp.float32) + inverse[rows, :] * inner).astype(jnp.bfloat16)

        @pl.when(s > 0)
        def _():
            cot_copy(c).start()

        sc_copy(c).start()

    def arrival(_):
        pl.when(alone)(functools.partial(arrive, value_lanes))

        @pl.when(helped)
        def _():
            @pl.loop(0, hops)
            def _(t):
                for k in value_lanes:
                    pl.when(travels(k, t))(lambda: back_copy(k, t).wait_recv())

        @pl.when(jnp.logical_not(leads))
        def _():
            tell_partner()

    def wg_copy(k):
        _, half, first, count, _ = streams[k]
        columns = pl.ds(half * hd + first, count)
        return pltpu.make_async_copy(wg_ref.at[:, columns], wg_hbm.at[:, columns], wg_sem.at[k])

    def ahead(direction, distance):
        return rows_of(lax.rem(place + direction * distance + n, n))

    def rs_copy(k, t, first_leg=False):
        direction, half, first, count, _ = streams[k]
        columns = pl.ds(first, count)
        side = (1 - direction) // 2
        if first_leg:
            origin = partial.at[half, ahead(direction, hops - t), columns]
        else:
            origin = landing.at[side, half, jnp.maximum(t - 1, 0), :, columns]
        return pltpu.make_async_remote_copy(
            src_ref=origin, dst_ref=landing.at[side, half, t, :, columns],
            send_sem=rs_send.at[k, t], recv_sem=rs_recv.at[k, t],
            device_id={"dp": up if direction == 1 else down}, device_id_type=MESH,
        )

    def send_partials(lanes):
        for k in sorted(lanes, key=lambda k: not streams[k][4]):
            rs_copy(k, 0 if streams[k][4] else 1, True).start()

    part = width // 2

    def gradients(half, b):
        rows = image_rows(b)

        @pl.loop(0, 2)
        def _(i):
            block = pl.ds(pl.multiple_of(i * part, 16), part)
            term = jnp.dot(
                lefts[half, block, rows], rights[half, rows, :],
                preferred_element_type=jnp.float32,
            )

            @pl.when(jnp.logical_and(b == 0, b < images - 1))
            def _():
                sums[half, block, :] = term

            @pl.when(jnp.logical_and(b > 0, b < images - 1))
            def _():
                sums[half, block, :] += term

            @pl.when(b == images - 1)
            def _():
                total = term if images == 1 else sums[half, block, :] + term
                partial[half, block, :] = total.astype(jnp.bfloat16)

    def cot_gradient(b):
        gradients(1, b)

        @pl.when(b == images - 1)
        def _():
            @pl.when(leads)
            def _():
                pl.semaphore_wait(go_sem, 1)

            send_partials(output_lanes)

    def norm_gradient(b):
        gradients(0, b)

        @pl.when(b == images - 1)
        def _():
            send_partials(value_lanes)

    early, middle, final = (packed(steps) for steps in schedules(images))
    words = [
        jnp.where(s == 0, c, jnp.where(jnp.logical_and(leads, jnp.logical_not(last)), b, a))
        for a, b, c in zip(early, middle, final)
    ]
    actions = (forward, to_context, to_values, to_input, cot_gradient, norm_gradient, arrival, receive)

    @pl.loop(0, len(schedules(images)[0]))
    def _(i):
        group, slot = i // 3, lax.rem(i, 3)
        word = words[0]
        for j in range(1, len(words)):
            word = jnp.where(group == j, words[j], word)
        code = jnp.where(slot == 0, word, jnp.where(slot == 1, word // SLOT, word // (SLOT * SLOT)))
        code = lax.rem(code, SLOT)
        work, argument = code // OP_SIZE, lax.rem(code, OP_SIZE)
        for number, action in enumerate(actions):
            pl.when(work == number)(functools.partial(action, argument))

    @pl.loop(1, hops)
    def _(t):
        def add_on(k):
            direction, half, first, count, _ = streams[k]
            columns = pl.ds(first, count)
            side = (1 - direction) // 2
            rs_copy(k, t - 1).wait_recv()
            total = landing[side, half, t - 1, :, columns].astype(jnp.float32) + partial[
                half, ahead(direction, hops - t), columns
            ].astype(jnp.float32)
            landing[side, half, t - 1, :, columns] = total.astype(jnp.bfloat16)
            rs_copy(k, t).start()

        for k in lanes_of:
            if streams[k][4]:
                add_on(k)
            else:
                pl.when(t > 1)(functools.partial(add_on, k))

    for k in lanes_of[::2]:
        _, half, first, count, _ = streams[k]
        columns = pl.ds(first, count)
        total = partial[half, rows_of(place), columns].astype(jnp.float32)
        for side in range(2):
            rs_copy(k + side, hops - 1).wait_recv()
            total += landing[side, half, hops - 1, :, columns].astype(jnp.float32)
        wg_ref[:, pl.ds(half * hd + first, count)] = total
        wg_copy(k).start()

    @pl.loop(0, hops)
    def _(t):
        for k in lanes_of:
            sent = travels(k, t) if k in output_lanes else jnp.logical_and(alone, travels(k, t))
            pl.when(sent)(lambda: ag_copy(k, t, False).wait_send())
            pl.when(travels(k, hops - 1 - t))(lambda: rs_copy(k, t).wait_send())

    @pl.when(helped)
    def _():
        for k in value_lanes[::2]:
            seed_copy(k).wait_send()

    @pl.when(helps)
    def _():
        @pl.loop(0, hops)
        def _(t):
            for k in value_lanes:
                @pl.when(travels(k, t))
                def _():
                    ring_copy(k, t, False).wait_send()
                    back_copy(k, t).wait_send()

    @pl.when(s > 0)
    def _():
        @pl.loop(0, images)
        def _(c):
            cot_copy(c).wait_send()

    @pl.loop(0, images)
    def _(c):
        sc_copy(c).wait()

    for k in lanes_of[::2]:
        wg_copy(k).wait()


def fused_body(saved_inputs, projections, mixing, out_cotangent):
    n = lax.axis_size("dp")
    rows, width = out_cotangent.shape
    share, both = projections.shape[1:]
    hd = both // 2
    images, heads, patches = mixing.shape[1:4]
    bf16, f32 = jnp.bfloat16, jnp.float32
    hbm = pl.BlockSpec(memory_space=pl.ANY)
    section_grads, weight_grads = pl.pallas_call(
        fused_kernel,
        out_shape=(
            jax.ShapeDtypeStruct((rows, width), bf16),
            jax.ShapeDtypeStruct((share, both), f32),
        ),
        in_specs=[hbm] * 4,
        out_specs=(hbm, hbm),
        scratch_shapes=[
            pltpu.VMEM((rows, width), bf16),
            pltpu.VMEM((images, heads, patches, patches), bf16),
            pltpu.VMEM((rows, width), bf16),
            pltpu.VMEM((share, both), f32),
            pltpu.VMEM((2, width, hd), f32),
            pltpu.VMEM((width, both), bf16),
            pltpu.VMEM((width, hd), bf16),
            pltpu.VMEM((rows, width), f32),
            pltpu.VMEM((rows, 1), f32),
            pltpu.VMEM((rows, width), bf16),
            pltpu.VMEM((2, width, rows), bf16),
            pltpu.VMEM((2, rows, hd), bf16),
            pltpu.VMEM((images, heads, patches, patches), bf16),
            pltpu.VMEM((rows, width), bf16),
            pltpu.VMEM((rows, hd), bf16),
            pltpu.VMEM((rows, hd), bf16),
            pltpu.VMEM((2, width, hd), bf16),
            pltpu.VMEM((2, 2, n // 2, share, hd), bf16),
            pltpu.SemaphoreType.DMA((8, n // 2)),
            pltpu.SemaphoreType.DMA((8, n // 2)),
            pltpu.SemaphoreType.DMA((8, n // 2)),
            pltpu.SemaphoreType.DMA((8, n // 2)),
            pltpu.SemaphoreType.DMA((rows // LANES,)),
            pltpu.SemaphoreType.DMA((rows // LANES,)),
            pltpu.SemaphoreType.DMA((4,)),
            pltpu.SemaphoreType.DMA((rows // LANES,)),
            pltpu.SemaphoreType.DMA((8,)),
            pltpu.SemaphoreType.DMA((2,)),
            pltpu.SemaphoreType.DMA((2,)),
            pltpu.SemaphoreType.DMA((4, n // 2)),
            pltpu.SemaphoreType.DMA((4, n // 2)),
            pltpu.SemaphoreType.DMA((4, n // 2)),
            pltpu.SemaphoreType.DMA((4, n // 2)),
            pltpu.SemaphoreType.REGULAR,
        ],
        compiler_params=pltpu.CompilerParams(
            collective_id=0, has_side_effects=True, vmem_limit_bytes=48 * 1024 * 1024
        ),
    )(*(pltpu.with_memory_space_constraint(a, pltpu.HBM) for a in (saved_inputs[0], projections[0], mixing[0], out_cotangent)))
    return (section_grads[None], weight_grads[None])


def any_body(saved_inputs, projections, mixing, out_cotangent):
    share, both = projections.shape[1:]
    width = saved_inputs.shape[2]
    n = lax.axis_size("dp")
    aligned = (
        share % 16 == 0
        and both % (2 * LANES) == 0
        and width % LANES == 0
        and mixing.shape[3] % LANES == 0
        and n % 2 == 0
        and n > 2
        and lax.axis_size("pipe") > 2
        and lax.axis_size("pipe") % 2 == 0
        and out_cotangent.shape[0] < OP_SIZE * LANES
    )
    chosen = fused_body if aligned else body
    return chosen(saved_inputs, projections, mixing, out_cotangent)


def solution(mesh):
    return jax.shard_map(
        any_body,
        mesh=mesh,
        in_specs=(
            P("pipe", "dp", None),
            P("pipe", "dp", None),
            P("pipe", "dp", None, None, None),
            P("dp", None),
        ),
        out_specs=(P("pipe", "dp", None), P("pipe", "dp", None)),
        check_vma=False,
    )
```
